256 devices in a mesh: own: 64 (over z, x, core), grp: 4 (over y).
Axes of the slice: x: 4, y: 4, z: 8, core: 2. Of those that a mesh axis runs over, the one named last changes fastest.
Arguments:
- panel: float32 [64, 4, 768, 768], P('own', 'grp'), may hold values from -6 to 6
- diag_inverse: float32 [64, 768, 768], P('own', 'grp'), as said below
- ancestor: float32 [64, 4, 768, 768], P('own', 'grp'), may hold values from -6 to 6
- live_blocks: int32 [64], P('own'), may hold values from 1 to 4
- pair_first: int32 [64, 4, 7], P('own', 'grp'), may hold values from 0 to 3
- pair_second: int32 [64, 4, 7], P('own', 'grp'), may hold values from 0 to 3
- pair_offset: int32 [64, 4, 7], P('own', 'grp'), may hold values from 0 to 4
Outputs:
- solved: float32 [64, 4, 768, 768], P('own', 'grp')
- updated: float32 [64, 4, 768, 768], P('own', 'grp')
The draws below stay inside these ranges and needn't reach their ends.
Inputs may be any that keep to these rules, and one draw needn't show every extreme that they name: diag_inverse[s] is upper triangular with a positive diagonal.
All inputs are finite; a program needn't handle non-finite values.
Results may differ from the reference program's by a relative error of at most 0.0001.
Values sent between devices are 32-bit elements; how exact they have to be, the bound alone decides.
A program may use at most 128 MiB of HBM per device.

```python
import math
import jax
import jax.numpy as jnp
import numpy as np
from jax import lax

B = 768
PAIRS = 7
REACH = 5
SUPERS = 64
N_GRP = 4


def draw_diag_inverse(key, part):
    first_key, second_key = jax.random.split(jax.random.fold_in(key, 71))
    factor = B ** (-0.25)
    diagonal = jax.random.uniform(first_key, (SUPERS, B), jnp.float32, 0.5, 1.0) * factor
    upper = jax.random.normal(second_key, (SUPERS, B, B), jnp.float32) * (factor / B ** 0.5)
    strict = jnp.triu(jnp.ones((B, B), jnp.float32), 1)
    return upper * strict[None] + diagonal[:, :, None] * jnp.eye(B, dtype=jnp.float32)[None]


def touch_ends(entries, stream_key, smallest, high):
    longest = entries.shape.index(max(entries.shape))
    spots = []
    for shift in (0, 1):
        where = [jax.random.randint(jax.random.fold_in(stream_key, axis), (), 0, length) for axis, length in enumerate(entries.shape)]
        where[longest] = (where[longest] + shift) % entries.shape[longest]
        spots.append(tuple(where))
    return entries.at[spots[0]].set(smallest).at[spots[1]].set(high)


def steps_of(own_key, dims, shards, low, largest):
    def one(axis_at, parts):
        heights = jax.random.uniform(jax.random.fold_in(jax.random.fold_in(own_key, 6), axis_at), (parts,), jnp.float32, low / len(shards), largest / len(shards))
        return jnp.repeat(jnp.exp(heights), dims[axis_at] // parts).reshape((-1,) + (1,) * (len(dims) - axis_at - 1))

    factor_of = one(*shards[0])
    for cut in shards[1:]:
        factor_of = factor_of * one(*cut)
    return factor_of


def rank_bounds(count, skew):
    portions = [(1 << 20) // math.isqrt(grade ** skew) + 1 for grade in range(1, count + 1)]
    spread = 1 + sum(portions) // (1 << 30)
    return np.cumsum(np.array([max(1, weight // spread) for weight in portions]))


def ranked_ids(stream_key, shape, count, skew):
    table = rank_bounds(count, skew)
    lot = jax.random.randint(jax.random.fold_in(stream_key, 1), shape, 0, int(table[count - 1]))
    standing = jnp.searchsorted(jnp.asarray(table, jnp.int32), lot, side="right")
    return jax.random.permutation(jax.random.fold_in(stream_key, 2), count)[standing].astype(jnp.int32)


def bell_draw(rng, shape, spread, reach, cuts=(), kind=jnp.bfloat16):
    result = jax.random.normal(rng, shape, jnp.float32) * spread
    if len(cuts) > 0:
        result = steps_of(rng, shape, cuts, -0.22, 0.18) * result
    return jnp.clip(result, min=-reach, max=reach).astype(kind)


def setup_inputs(seed: int = 0) -> dict:
    arg_keys = jax.random.split(jax.random.key(seed), 8)
    panel = bell_draw(arg_keys[0], (SUPERS, N_GRP, B, B), 1.0, 6.0, ((0, 64), (1, 4)), jnp.float32)
    diag_inverse = draw_diag_inverse(jax.random.fold_in(arg_keys[7], 71), 0)
    ancestor = bell_draw(arg_keys[2], (SUPERS, N_GRP, B, B), 1.0, 6.0, ((0, 64), (1, 4)), jnp.float32)
    live_blocks = touch_ends(jax.random.randint(arg_keys[3], (SUPERS,), 1, N_GRP + 1), jax.random.fold_in(arg_keys[3], 1), 1, N_GRP).astype(jnp.int32)
    pair_first = touch_ends(jax.random.randint(arg_keys[4], (SUPERS, N_GRP, PAIRS), 0, N_GRP), jax.random.fold_in(arg_keys[4], 1), 0, N_GRP - 1).astype(jnp.int32)
    pair_second = touch_ends(jax.random.randint(arg_keys[5], (SUPERS, N_GRP, PAIRS), 0, N_GRP), jax.random.fold_in(arg_keys[5], 1), 0, N_GRP - 1).astype(jnp.int32)
    pair_offset = touch_ends(ranked_ids(arg_keys[6], (SUPERS, N_GRP, PAIRS), REACH, 2), jax.random.fold_in(arg_keys[6], 3), 0, REACH - 1).astype(jnp.int32)
    return {"panel": panel, "diag_inverse": diag_inverse, "ancestor": ancestor, "live_blocks": live_blocks, "pair_first": pair_first, "pair_second": pair_second, "pair_offset": pair_offset}


def reference(panel, diag_inverse, ancestor, live_blocks, pair_first, pair_second, pair_offset):
    groups = panel.shape[1]
    alive = (jnp.arange(groups, dtype=jnp.int32)[None, :] < live_blocks[:, None]).astype(panel.dtype)
    solved = jnp.einsum("sgij,sjk->sgik", panel, diag_inverse, precision=lax.Precision.HIGHEST)
    solved = solved * alive[:, :, None, None]
    supers = panel.shape[0]

    def one_super(index, updated):
        column = solved[index]
        first = column[pair_first[index]]
        second = column[pair_second[index]]
        terms = jnp.einsum("gpij,gpkj->gpik", first, second, precision=lax.Precision.HIGHEST)
        for distance in range(REACH):
            weights = (pair_offset[index] == distance).astype(terms.dtype)
            contrib = jnp.einsum("gp,gpik->gik", weights, terms, precision=lax.Precision.HIGHEST)
            target = ((index + distance) % supers).astype(jnp.int32)
            current = lax.dynamic_index_in_dim(updated, target, 0, keepdims=False)
            updated = lax.dynamic_update_index_in_dim(updated, current - contrib, target, 0)
        return updated

    updated = lax.fori_loop(0, supers, one_super, ancestor)
    return solved, updated
```

```python
import jax
import jax.numpy as jnp
from jax import lax
from jax.experimental import pallas as pl
from jax.experimental.pallas import tpu as pltpu
from jax.sharding import PartitionSpec as P

MESH = pl.DeviceIdType.MESH
B = 768
PAIRS = 7
R = 128
C = B // R
TILES = C * C
SLAB = B // 4
GROUPS = ((0, 128, 1), (128, 256, 2), (384, 128, 3), (512, 256, 4))
NT = (((1,), (1,)), ((), ()))


def split(x):
    hi = x.astype(jnp.bfloat16)
    lo = (x - hi.astype(jnp.float32)).astype(jnp.bfloat16)
    return hi, lo


def kernel(
    live, first, second, offset, panel, diag, anc,
    solved_out, updated_out,
    factor, fac_hi, fac_lo, rows, solved, gath, halves, out, part, xin, base, upd, terms,
    local_sem, fac_send, fac_recv, near_send, near_recv, fwd_send, fwd_recv,
    part_send, part_recv, one_send, one_recv, two_send, two_recv,
):
    own = lax.axis_index("own")
    grp = lax.axis_index("grp")
    core = lax.rem(own, 2)

    def dev(by_own, by_grp):
        return (lax.rem(own + by_own + 64, 64), lax.rem(grp + by_grp + 4, 4))

    partner = (own + 1 - 2 * core, grp)
    up, down, across = dev(0, 1), dev(0, -1), dev(0, 2)

    load_rows = pltpu.make_async_copy(panel.at[0, 0], rows, local_sem.at[0])
    load_base = pltpu.make_async_copy(anc.at[0, 0], base, local_sem.at[1])
    load_rows.start()
    load_base.start()
    barrier = pltpu.get_barrier_semaphore()
    peers = (up, down, across, partner, dev(2, 0), dev(-2, 0), dev(4, 0), dev(-4, 0))
    for peer in peers:
        pl.semaphore_signal(barrier, 1, device_id=peer, device_id_type=MESH)
    pl.semaphore_wait(barrier, len(peers))

    def slab_copy(which, group, source_slab, target):
        start, width, _ = GROUPS[group]
        place = factor.at[pl.ds(pl.multiple_of(source_slab * SLAB, SLAB), SLAB), pl.ds(start, width)]
        return pltpu.make_async_remote_copy(
            diag.at[0, :, pl.ds(start, width)], place,
            fac_send.at[which, group], fac_recv.at[which, group],
            device_id=target, device_id_type=MESH,
        )

    for group in range(4):
        @pl.when(grp < GROUPS[group][2])
        def _():
            for which, target in enumerate((up, across, down)):
                slab_copy(which, group, grp, target).start()

    load_slab = pltpu.make_async_copy(
        diag.at[0], factor.at[pl.ds(pl.multiple_of(grp * SLAB, SLAB), SLAB)], local_sem.at[2]
    )
    load_slab.start()
    load_slab.wait()
    for group in range(4):
        for which, by in enumerate((3, 2, 1)):
            source = lax.rem(grp + by, 4)

            @pl.when(source < GROUPS[group][2])
            def _():
                slab_copy(which, group, source, up).wait_recv()
    load_rows.wait()

    def split_factor(c, _):
        at = pl.ds(pl.multiple_of(c * R, R), R)
        row = lax.broadcasted_iota(jnp.int32, (R, B), 0) + c * R
        col = lax.broadcasted_iota(jnp.int32, (R, B), 1)
        hi, lo = split(jnp.where(row <= col, factor[at, :], 0.0))
        fac_hi[at, :] = hi
        fac_lo[at, :] = lo
        return 0

    lax.fori_loop(0, C, split_factor, 0)
    alive = (grp < live[0]).astype(jnp.float32)

    def near_copy(side, c):
        at = pl.ds(pl.multiple_of(c * R, R), R)
        return pltpu.make_async_remote_copy(
            solved.at[at], gath.at[2 if side == 0 else 0, at],
            near_send.at[side, c], near_recv.at[side, c],
            device_id=up if side == 0 else down, device_id_type=MESH,
        )

    def fwd_copy(side, c):
        at = pl.ds(pl.multiple_of(c * R + side * (R // 2), R // 2), R // 2)
        return pltpu.make_async_remote_copy(
            gath.at[2 if side == 0 else 0, at], gath.at[1, at],
            fwd_send.at[side, c], fwd_recv.at[side, c],
            device_id=up if side == 0 else down, device_id_type=MESH,
        )

    def put_halves(slot, c, x):
        hi, lo = split(x)
        halves[slot, pl.ds(pl.multiple_of(c * 2 * R, 2 * R), R), :] = hi
        halves[slot, pl.ds(pl.multiple_of(c * 2 * R + R, R), R), :] = lo

    def solve_send(c):
        at = pl.ds(pl.multiple_of(c * R, R), R)
        hi, lo = split(rows[at, :])
        both = jnp.concatenate([hi, lo], axis=0)
        for j in range(3):
            k = 256 * (j + 1)
            cols = pl.ds(256 * j, 256)
            x = jnp.dot(both[:, :k], fac_hi[pl.ds(0, k), cols], preferred_element_type=jnp.float32)
            y = jnp.dot(hi[:, :k], fac_lo[pl.ds(0, k), cols], preferred_element_type=jnp.float32)
            solved[at, cols] = alive * (x[:R] + (x[R:] + y))
        near_copy(0, c).start()
        near_copy(1, c).start()
        put_halves(0, c, solved[at, :])

    def near_wait_forward(c):
        near_copy(0, c).wait_recv()
        fwd_copy(0, c).start()
        near_copy(1, c).wait_recv()
        fwd_copy(1, c).start()

    def first_two(c, _):
        solve_send(c)
        return 0

    lax.fori_loop(0, 2, first_two, 0)
    near_wait_forward(0)

    lefts = [lax.rem(first[0, 0, p] - grp + 4, 4) for p in range(PAIRS)]
    rights = [lax.rem(second[0, 0, p] - grp + 4, 4) for p in range(PAIRS)]
    dists = (3 - 2 * core, 1 + 2 * core, 2, 4, 0)
    weights = [
        [(offset[0, 0, p] == d).astype(jnp.float32) for p in range(PAIRS)] for d in dists
    ]

    def part_copy(n):
        return pltpu.make_async_remote_copy(
            out.at[n, pl.ds(0, 2)], part.at[n], part_send.at[n], part_recv.at[n],
            device_id=partner, device_id_type=MESH,
        )

    def one_copy(n):
        return pltpu.make_async_remote_copy(
            out.at[n, 2], xin.at[n, 0], one_send.at[n], one_recv.at[n],
            device_id=dev(2, 0), device_id_type=MESH,
        )

    def two_copy(n):
        return pltpu.make_async_remote_copy(
            out.at[n, 3], xin.at[n, 1], two_send.at[n], two_recv.at[n],
            device_id=dev(4, 0), device_id_type=MESH,
        )

    def combine_send(n):
        part_copy(n).wait_recv()
        out[n, 2] = out[n, 2] + part[n, 0]
        one_copy(n).start()
        out[n, 3 + core] = out[n, 3 + core] + part[n, 1]
        two_copy(n).start()

    def tile(c, k):
        n = c * c + k
        is_row = k <= c
        i = jnp.where(is_row, c, k - c - 1)
        j = jnp.where(is_row, k, c)
        at_i = pl.ds(pl.multiple_of(i * 2 * R, 2 * R), 2 * R)
        at_j = pl.ds(pl.multiple_of(j * 2 * R, 2 * R), 2 * R)
        for p in range(PAIRS):
            x = lax.dot_general(
                halves[lefts[p], at_i, :], halves[rights[p], at_j, :], NT,
                preferred_element_type=jnp.float32,
            )
            terms[p] = (x[:R, :R] + (x[R:, :R] + x[:R, R:])) + x[R:, R:]
        def mix(r, _):
            at = pl.ds(pl.multiple_of(r * 16, 16), 16)
            t = [terms[p, at, :] for p in range(PAIRS)]
            for slot in range(5):
                w = weights[slot]
                total = w[0] * t[0]
                for p in range(1, PAIRS):
                    total = total + w[p] * t[p]
                out[n, slot, at, :] = total
            return 0

        lax.fori_loop(0, R // 16, mix, 0, unroll=True)
        part_copy(n).start()

        @pl.when(k > 0)
        def _():
            combine_send(n - 1)

    def step(c, _):
        @pl.when(c + 2 < C)
        def _():
            solve_send(c + 2)

        @pl.when(c + 1 < C)
        def _():
            near_wait_forward(c + 1)

        at = pl.ds(pl.multiple_of(c * R, R), R)
        put_halves(1, c, gath[0, at, :])
        put_halves(3, c, gath[2, at, :])
        fwd_copy(0, c).wait_recv()
        fwd_copy(1, c).wait_recv()
        put_halves(2, c, gath[1, at, :])

        def one_tile(k, _):
            tile(c, k)
            return 0

        lax.fori_loop(0, 2 * c + 1, one_tile, 0)
        combine_send(c * c + 2 * c)
        return 0

    lax.fori_loop(0, C, step, 0)
    store_solved = pltpu.make_async_copy(solved, solved_out.at[0, 0], local_sem.at[0])
    store_solved.start()
    load_base.wait()

    def finish(c, _):
        def one(k, _):
            n = c * c + k
            is_row = k <= c
            i = jnp.where(is_row, c, k - c - 1)
            j = jnp.where(is_row, k, c)
            at_i = pl.ds(pl.multiple_of(i * R, R), R)
            at_j = pl.ds(pl.multiple_of(j * R, R), R)
            one_copy(n).wait_recv()
            two_copy(n).wait_recv()
            upd[at_i, at_j] = base[at_i, at_j] - (out[n, 4] + (xin[n, 0] + xin[n, 1]))
            return 0

        lax.fori_loop(0, 2 * c + 1, one, 0)
        return 0

    lax.fori_loop(0, C, finish, 0)
    store_updated = pltpu.make_async_copy(upd, updated_out.at[0, 0], local_sem.at[1])
    store_updated.start()

    for group in range(4):
        @pl.when(grp < GROUPS[group][2])
        def _():
            for which, target in enumerate((up, across, down)):
                slab_copy(which, group, grp, target).wait_send()

    def drain_chunk(c, _):
        for side in range(2):
            near_copy(side, c).wait_send()
            fwd_copy(side, c).wait_send()
        return 0

    def drain_tile(n, _):
        part_copy(n).wait_send()
        one_copy(n).wait_send()
        two_copy(n).wait_send()
        return 0

    lax.fori_loop(0, C, drain_chunk, 0)
    lax.fori_loop(0, TILES, drain_tile, 0)
    store_solved.wait()
    store_updated.wait()


def shards(panel, diag_inverse, ancestor, live_blocks, pair_first, pair_second, pair_offset):
    f32, bf16 = jnp.float32, jnp.bfloat16
    dma = pltpu.SemaphoreType.DMA
    smem = pl.BlockSpec(memory_space=pltpu.SMEM)
    raw = pl.BlockSpec(memory_space=pl.ANY)
    block = jax.ShapeDtypeStruct((1, 1, B, B), f32)
    return pl.pallas_call(
        kernel,
        out_shape=(block, block),
        in_specs=[smem] * 4 + [raw] * 3,
        out_specs=(raw, raw),
        scratch_shapes=[
            pltpu.VMEM((B, B), f32),
            pltpu.VMEM((B, B), bf16),
            pltpu.VMEM((B, B), bf16),
            pltpu.VMEM((B, B), f32),
            pltpu.VMEM((B, B), f32),
            pltpu.VMEM((3, B, B), f32),
            pltpu.VMEM((4, 2 * B, B), bf16),
            pltpu.VMEM((TILES, 5, R, R), f32),
            pltpu.VMEM((TILES, 2, R, R), f32),
            pltpu.VMEM((TILES, 2, R, R), f32),
            pltpu.VMEM((B, B), f32),
            pltpu.VMEM((B, B), f32),
            pltpu.VMEM((PAIRS, R, R), f32),
            dma((3,)),
            dma((3, 4)),
            dma((3, 4)),
            dma((2, C)),
            dma((2, C)),
            dma((2, C)),
            dma((2, C)),
            dma((TILES,)),
            dma((TILES,)),
            dma((TILES,)),
            dma((TILES,)),
            dma((TILES,)),
            dma((TILES,)),
        ],
        compiler_params=pltpu.CompilerParams(
            collective_id=0, has_side_effects=True, vmem_limit_bytes=60 * 2**20
        ),
    )(live_blocks, pair_first, pair_second, pair_offset, panel, diag_inverse, ancestor)


def solution(mesh):
    placed = (
        P("own", "grp", None, None),
        P("own", "grp", None),
        P("own", "grp", None, None),
        P("own"),
        P("own", "grp", None),
        P("own", "grp", None),
        P("own", "grp", None),
    )
    return jax.shard_map(
        shards,
        mesh=mesh,
        in_specs=placed,
        out_specs=(P("own", "grp", None, None), P("own", "grp", None, None)),
        check_vma=False,
    )
```

```python
import jax
import jax.numpy as jnp
from jax import lax
from jax.experimental import pallas as pl
from jax.experimental.pallas import tpu as pltpu
from jax.sharding import PartitionSpec as P

MESH = pl.DeviceIdType.MESH
B = 768
PAIRS = 7
R = 128
C = B // R
H = R // 2
TILES = C * C
MID = 4
SLAB = B // 4
GROUPS = ((0, 128, 1), (128, 256, 2), (384, 128, 3), (512, 256, 4))
NT = (((1,), (1,)), ((), ()))


def split(x):
    hi = x.astype(jnp.bfloat16)
    lo = (x - hi.astype(jnp.float32)).astype(jnp.bfloat16)
    return hi, lo


def kernel(
    live, first, second, offset, panel, diag, anc,
    solved_out, updated_out,
    factor, fac_hi, fac_lo, rows, solved, mine, gath, halves, out, part, xin, base, upd, terms,
    packed, pairs_in, pairs, local_sem, pairs_sem, fac_send, fac_recv, shift_send, shift_recv,
    near_send, near_recv, fwd_send, fwd_recv, part_send, part_recv, low_send, low_recv, high_send, high_recv,
):
    own = lax.axis_index("own")
    grp = lax.axis_index("grp")
    core = lax.rem(own, 2)

    def dev(by_own, by_grp):
        return (lax.rem(own + by_own + 64, 64), lax.rem(grp + by_grp + 4, 4))

    partner = (own + 1 - 2 * core, grp)
    up, down, across = dev(0, 1), dev(0, -1), dev(0, 2)

    load_rows = pltpu.make_async_copy(panel.at[0, 0], rows, local_sem.at[0])
    load_base = pltpu.make_async_copy(anc.at[0, 0], base, local_sem.at[1])
    load_rows.start()
    load_base.start()
    barrier = pltpu.get_barrier_semaphore()
    after, before = dev(2, 0), dev(-2, 0)
    peers = (up, down, across, partner, after, before)
    for peer in peers:
        pl.semaphore_signal(barrier, 1, device_id=peer, device_id_type=MESH)
    pl.semaphore_wait(barrier, len(peers))

    def slab_copy(which, group, source_slab, target):
        start, width, _ = GROUPS[group]
        place = factor.at[pl.ds(pl.multiple_of(source_slab * SLAB, SLAB), SLAB), pl.ds(start, width)]
        return pltpu.make_async_remote_copy(
            diag.at[0, :, pl.ds(start, width)], place,
            fac_send.at[which, group], fac_recv.at[which, group],
            device_id=target, device_id_type=MESH,
        )

    for group in range(4):
        @pl.when(grp < GROUPS[group][2])
        def _():
            for which, target in enumerate((up, across, down)):
                slab_copy(which, group, grp, target).start()

    spot = lax.broadcasted_iota(jnp.int32, (8, 128), 1) + 128 * lax.broadcasted_iota(jnp.int32, (8, 128), 0)
    values = jnp.zeros((8, 128), jnp.int32)
    for row, source in enumerate((first, second, offset)):
        for p in range(PAIRS):
            values = jnp.where(spot == 128 * row + p, source[0, 0, p], values)
    packed[...] = values
    pairs_copy = pltpu.make_async_remote_copy(
        packed, pairs_in, pairs_sem.at[0], pairs_sem.at[1], device_id=after, device_id_type=MESH
    )
    pairs_copy.start()

    load_slab = pltpu.make_async_copy(
        diag.at[0], factor.at[pl.ds(pl.multiple_of(grp * SLAB, SLAB), SLAB)], local_sem.at[2]
    )
    load_slab.start()
    load_slab.wait()
    for group in range(4):
        for which, by in enumerate((3, 2, 1)):
            source = lax.rem(grp + by, 4)

            @pl.when(source < GROUPS[group][2])
            def _():
                slab_copy(which, group, source, up).wait_recv()
    load_rows.wait()

    def split_factor(c, _):
        at = pl.ds(pl.multiple_of(c * R, R), R)
        row = lax.broadcasted_iota(jnp.int32, (R, B), 0) + c * R
        col = lax.broadcasted_iota(jnp.int32, (R, B), 1)
        hi, lo = split(jnp.where(row <= col, factor[at, :], 0.0))
        fac_hi[at, :] = hi
        fac_lo[at, :] = lo
        return 0

    lax.fori_loop(0, C, split_factor, 0)
    alive = (grp < live[0]).astype(jnp.float32)

    def shift_copy(m):
        at = pl.ds(pl.multiple_of(m * H, H), H)
        return pltpu.make_async_remote_copy(
            solved.at[at], mine.at[at], shift_send.at[m], shift_recv.at[m],
            device_id=after, device_id_type=MESH,
        )

    def near_copy(side, m):
        at = pl.ds(pl.multiple_of(m * H, H), H)
        return pltpu.make_async_remote_copy(
            mine.at[at], gath.at[2 if side == 0 else 0, at],
            near_send.at[side, m], near_recv.at[side, m],
            device_id=up if side == 0 else down, device_id_type=MESH,
        )

    def fwd_copy(side, c):
        at = pl.ds(pl.multiple_of(c * R + side * H, H), H)
        return pltpu.make_async_remote_copy(
            gath.at[2 if side == 0 else 0, at], gath.at[1, at],
            fwd_send.at[side, c], fwd_recv.at[side, c],
            device_id=up if side == 0 else down, device_id_type=MESH,
        )

    def put_halves(slot, c, x):
        hi, lo = split(x)
        halves[slot, pl.ds(pl.multiple_of(c * 2 * R, 2 * R), R), :] = hi
        halves[slot, pl.ds(pl.multiple_of(c * 2 * R + R, R), R), :] = lo

    def solve_shift(c, _):
        at = pl.ds(pl.multiple_of(c * R, R), R)
        hi, lo = split(rows[at, :])
        both = jnp.concatenate([hi, lo], axis=0)
        for j in range(3):
            k = 256 * (j + 1)
            cols = pl.ds(256 * j, 256)
            x = jnp.dot(both[:, :k], fac_hi[pl.ds(0, k), cols], preferred_element_type=jnp.float32)
            y = jnp.dot(hi[:, :k], fac_lo[pl.ds(0, k), cols], preferred_element_type=jnp.float32)
            solved[at, cols] = alive * (x[:R] + (x[R:] + y))
        shift_copy(2 * c).start()
        shift_copy(2 * c + 1).start()
        return 0

    def near_start(c):
        shift_copy(2 * c).wait_recv()
        near_copy(0, 2 * c).start()
        shift_copy(2 * c + 1).wait_recv()
        near_copy(1, 2 * c + 1).start()
        near_copy(0, 2 * c + 1).start()
        near_copy(1, 2 * c).start()
        put_halves(0, c, mine[pl.ds(pl.multiple_of(c * R, R), R), :])

    def forward(c):
        near_copy(0, 2 * c).wait_recv()
        fwd_copy(0, c).start()
        near_copy(1, 2 * c + 1).wait_recv()
        fwd_copy(1, c).start()

    lax.fori_loop(0, C, solve_shift, 0)
    store_solved = pltpu.make_async_copy(solved, solved_out.at[0, 0], local_sem.at[0])
    store_solved.start()
    near_start(0)
    pairs_copy.wait_recv()
    load_pairs = pltpu.make_async_copy(pairs_in, pairs, local_sem.at[2])
    load_pairs.start()
    load_pairs.wait()
    forward(0)
    near_start(1)

    lefts = [lax.rem(pairs[0, p] - grp + 4, 4) for p in range(PAIRS)]
    rights = [lax.rem(pairs[1, p] - grp + 4, 4) for p in range(PAIRS)]
    dists = (1 + 2 * core, 3 - 2 * core, 0, 4, 2)
    weights = [
        [(pairs[2, p] == d).astype(jnp.float32) for p in range(PAIRS)] for d in dists
    ]

    def part_copy(n):
        return pltpu.make_async_remote_copy(
            out.at[n, pl.ds(0, 2)], part.at[n], part_send.at[n], part_recv.at[n],
            device_id=partner, device_id_type=MESH,
        )

    def low_copy(n):
        return pltpu.make_async_remote_copy(
            out.at[n, 2], xin.at[n, 0], low_send.at[n], low_recv.at[n],
            device_id=before, device_id_type=MESH,
        )

    def high_copy(n):
        return pltpu.make_async_remote_copy(
            out.at[n, 3], xin.at[n, 1], high_send.at[n], high_recv.at[n],
            device_id=after, device_id_type=MESH,
        )

    def combine_send(n):
        part_copy(n).wait_recv()
        out[n, 3 - core] = out[n, 3 - core] + part[n, 0]
        low_copy(n).start()
        high_copy(n).start()
        out[n, 4] = out[n, 4] + part[n, 1]

    def tile(c, k):
        n = c * c + k
        is_row = k <= c
        i = jnp.where(is_row, c, k - c - 1)
        j = jnp.where(is_row, k, c)
        at_i = pl.ds(pl.multiple_of(i * 2 * R, 2 * R), 2 * R)
        at_j = pl.ds(pl.multiple_of(j * 2 * R, 2 * R), 2 * R)
        for p in range(PAIRS):
            x = lax.dot_general(
                halves[lefts[p], at_i, :], halves[rights[p], at_j, :], NT,
                preferred_element_type=jnp.float32,
            )
            terms[p] = (x[:R, :R] + (x[R:, :R] + x[:R, R:])) + x[R:, R:]
        def mix(r, _):
            at = pl.ds(pl.multiple_of(r * 16, 16), 16)
            t = [terms[p, at, :] for p in range(PAIRS)]
            for slot in range(5):
                w = weights[slot]
                total = w[0] * t[0]
                for p in range(1, PAIRS):
                    total = total + w[p] * t[p]
                out[n, slot, at, :] = total
            return 0

        lax.fori_loop(0, R // 16, mix, 0, unroll=True)
        part_copy(n).start()

        @pl.when(k > 0)
        def _():
            combine_send(n - 1)

    def finish(c):
        def one(k, _):
            n = c * c + k
            is_row = k <= c
            i = jnp.where(is_row, c, k - c - 1)
            j = jnp.where(is_row, k, c)
            at_i = pl.ds(pl.multiple_of(i * R, R), R)
            at_j = pl.ds(pl.multiple_of(j * R, R), R)
            low_copy(n).wait_recv()
            high_copy(n).wait_recv()
            upd[at_i, at_j] = base[at_i, at_j] - (out[n, 4] + (xin[n, 0] + xin[n, 1]))
            return 0

        lax.fori_loop(0, 2 * c + 1, one, 0)

    load_base.wait()

    def step(c, _):
        @pl.when(c >= 2)
        def _():
            finish(c - 2)

        at = pl.ds(pl.multiple_of(c * R, R), R)
        near_copy(0, 2 * c + 1).wait_recv()
        near_copy(1, 2 * c).wait_recv()
        put_halves(1, c, gath[0, at, :])
        put_halves(3, c, gath[2, at, :])
        fwd_copy(0, c).wait_recv()
        fwd_copy(1, c).wait_recv()
        put_halves(2, c, gath[1, at, :])

        def one_tile(k, _):
            tile(c, k)

            @pl.when(jnp.logical_and(k == jnp.minimum(MID, 2 * c), c + 1 < C))
            def _():
                forward(c + 1)

                @pl.when(c + 2 < C)
                def _():
                    near_start(c + 2)

            return 0

        lax.fori_loop(0, 2 * c + 1, one_tile, 0)
        combine_send(c * c + 2 * c)
        return 0

    lax.fori_loop(0, C, step, 0)
    finish(C - 2)
    edge = B - R
    stores = [
        pltpu.make_async_copy(upd.at[pl.ds(r, h), pl.ds(c, w)], updated_out.at[0, 0, pl.ds(r, h), pl.ds(c, w)], sem)
        for r, h, c, w, sem in (
            (0, edge, 0, edge, local_sem.at[1]), (edge, R, 0, B, local_sem.at[2]), (0, edge, edge, R, local_sem.at[3])
        )
    ]
    stores[0].start()
    finish(C - 1)
    stores[1].start()
    stores[2].start()

    for group in range(4):
        @pl.when(grp < GROUPS[group][2])
        def _():
            for which, target in enumerate((up, across, down)):
                slab_copy(which, group, grp, target).wait_send()

    pairs_copy.wait_send()

    def drain_piece(m, _):
        shift_copy(m).wait_send()
        for side in range(2):
            near_copy(side, m).wait_send()
        return 0

    def drain_chunk(c, _):
        for side in range(2):
            fwd_copy(side, c).wait_send()
        return 0

    def drain_tile(n, _):
        part_copy(n).wait_send()
        low_copy(n).wait_send()
        high_copy(n).wait_send()
        return 0

    lax.fori_loop(0, 2 * C, drain_piece, 0)
    lax.fori_loop(0, C, drain_chunk, 0)
    lax.fori_loop(0, TILES, drain_tile, 0)
    store_solved.wait()
    for store in stores:
        store.wait()


def shards(panel, diag_inverse, ancestor, live_blocks, pair_first, pair_second, pair_offset):
    f32, bf16 = jnp.float32, jnp.bfloat16
    dma = pltpu.SemaphoreType.DMA
    smem = pl.BlockSpec(memory_space=pltpu.SMEM)
    raw = pl.BlockSpec(memory_space=pl.ANY)
    block = jax.ShapeDtypeStruct((1, 1, B, B), f32)
    return pl.pallas_call(
        kernel,
        out_shape=(block, block),
        in_specs=[smem] * 4 + [raw] * 3,
        out_specs=(raw, raw),
        scratch_shapes=[
            pltpu.VMEM((B, B), f32),
            pltpu.VMEM((B, B), bf16),
            pltpu.VMEM((B, B), bf16),
            pltpu.VMEM((B, B), f32),
            pltpu.VMEM((B, B), f32),
            pltpu.VMEM((B, B), f32),
            pltpu.VMEM((3, B, B), f32),
            pltpu.VMEM((4, 2 * B, B), bf16),
            pltpu.VMEM((TILES, 5, R, R), f32),
            pltpu.VMEM((TILES, 2, R, R), f32),
            pltpu.VMEM((TILES, 2, R, R), f32),
            pltpu.VMEM((B, B), f32),
            pltpu.VMEM((B, B), f32),
            pltpu.VMEM((PAIRS, R, R), f32),
            pltpu.VMEM((8, 128), jnp.int32),
            pltpu.VMEM((8, 128), jnp.int32),
            pltpu.SMEM((8, 128), jnp.int32),
            dma((4,)),
            dma((2,)),
            dma((3, 4)),
            dma((3, 4)),
            dma((2 * C,)),
            dma((2 * C,)),
            dma((2, 2 * C)),
            dma((2, 2 * C)),
            dma((2, C)),
            dma((2, C)),
            dma((TILES,)),
            dma((TILES,)),
            dma((TILES,)),
            dma((TILES,)),
            dma((TILES,)),
            dma((TILES,)),
        ],
        compiler_params=pltpu.CompilerParams(
            collective_id=0, has_side_effects=True, vmem_limit_bytes=60 * 2**20
        ),
    )(live_blocks, pair_first, pair_second, pair_offset, panel, diag_inverse, ancestor)


def solution(mesh):
    placed = (
        P("own", "grp", None, None),
        P("own", "grp", None),
        P("own", "grp", None, None),
        P("own"),
        P("own", "grp", None),
        P("own", "grp", None),
        P("own", "grp", None),
    )
    return jax.shard_map(
        shards,
        mesh=mesh,
        in_specs=placed,
        out_specs=(P("own", "grp", None, None), P("own", "grp", None, None)),
        check_vma=False,
    )
```

```python
import jax
import jax.numpy as jnp
from jax import lax
from jax.experimental import pallas as pl
from jax.experimental.pallas import tpu as pltpu
from jax.sharding import PartitionSpec as P

MESH = pl.DeviceIdType.MESH
B = 768
PAIRS = 7
R = 128
C = B // R
H = R // 2
TILES = C * C
MID = 4
AHEAD = 2
LAG = 2
SLAB = B // 4
GROUPS = ((0, 128, 1), (128, 256, 2), (384, 128, 3), (512, 256, 4))
NT = (((1,), (1,)), ((), ()))


def split(x):
    hi = x.astype(jnp.bfloat16)
    lo = (x - hi.astype(jnp.float32)).astype(jnp.bfloat16)
    return hi, lo


def kernel(
    live, first, second, offset, panel, diag, anc,
    solved_out, updated_out,
    factor, fac_hi, fac_lo, rows, solved, mine, gath, halves, out, part, xin, base, upd, terms,
    packed, pairs_in, pairs, local_sem, pairs_sem, fac_send, fac_recv, shift_send, shift_recv,
    near_send, near_recv, fwd_send, fwd_recv, part_send, part_recv, low_send, low_recv, high_send, high_recv,
):
    own = lax.axis_index("own")
    grp = lax.axis_index("grp")
    core = lax.rem(own, 2)

    def dev(by_own, by_grp):
        return (lax.rem(own + by_own + 64, 64), lax.rem(grp + by_grp + 4, 4))

    partner = (own + 1 - 2 * core, grp)
    up, down = dev(0, 1), dev(0, -1)

    load_rows = pltpu.make_async_copy(panel.at[0, 0], rows, local_sem.at[0])
    load_base = pltpu.make_async_copy(anc.at[0, 0], base, local_sem.at[1])
    load_rows.start()
    load_base.start()
    barrier = pltpu.get_barrier_semaphore()
    after, before = dev(2, 0), dev(-2, 0)
    peers = (up, down, partner, after, before)
    for peer in peers:
        pl.semaphore_signal(barrier, 1, device_id=peer, device_id_type=MESH)
    pl.semaphore_wait(barrier, len(peers))

    def slab_fwd(side, group, slab):
        start, width, _ = GROUPS[group]
        at = pl.multiple_of(slab * SLAB + side * (SLAB // 2), SLAB // 2)
        place = factor.at[pl.ds(at, SLAB // 2), pl.ds(start, width)]
        return pltpu.make_async_remote_copy(
            place, place, fac_send.at[2 + side, group], fac_recv.at[2 + side, group],
            device_id=up if side == 0 else down, device_id_type=MESH,
        )

    def slab_copy(which, group, source_slab, target):
        start, width, _ = GROUPS[group]
        place = factor.at[pl.ds(pl.multiple_of(source_slab * SLAB, SLAB), SLAB), pl.ds(start, width)]
        return pltpu.make_async_remote_copy(
            diag.at[0, :, pl.ds(start, width)], place,
            fac_send.at[which, group], fac_recv.at[which, group],
            device_id=target, device_id_type=MESH,
        )

    for group in (3, 1, 2, 0):
        @pl.when(grp < GROUPS[group][2])
        def _():
            for which, target in enumerate((up, down)):
                slab_copy(which, group, grp, target).start()

    spot = lax.broadcasted_iota(jnp.int32, (8, 128), 1) + 128 * lax.broadcasted_iota(jnp.int32, (8, 128), 0)
    values = jnp.zeros((8, 128), jnp.int32)
    for row, source in enumerate((first, second, offset)):
        for p in range(PAIRS):
            values = jnp.where(spot == 128 * row + p, source[0, 0, p], values)
    packed[...] = values
    pairs_copy = pltpu.make_async_remote_copy(
        packed, pairs_in, pairs_sem.at[0], pairs_sem.at[1], device_id=after, device_id_type=MESH
    )
    pairs_copy.start()

    load_slab = pltpu.make_async_copy(
        diag.at[0], factor.at[pl.ds(pl.multiple_of(grp * SLAB, SLAB), SLAB)], local_sem.at[2]
    )
    load_slab.start()
    below, above, opposite = (lax.rem(grp + by, 4) for by in (3, 1, 2))
    for group in (3, 1, 2, 0):
        for side, slab in enumerate((below, above)):
            @pl.when(slab < GROUPS[group][2])
            def _():
                slab_copy(side, group, slab, up).wait_recv()
                slab_fwd(side, group, slab).start()

    load_slab.wait()
    for group in (3, 1, 2, 0):
        @pl.when(opposite < GROUPS[group][2])
        def _():
            for side in range(2):
                slab_fwd(side, group, opposite).wait_recv()
    load_rows.wait()

    def split_factor(c, _):
        at = pl.ds(pl.multiple_of(c * R, R), R)
        row = lax.broadcasted_iota(jnp.int32, (R, B), 0) + c * R
        col = lax.broadcasted_iota(jnp.int32, (R, B), 1)
        hi, lo = split(jnp.where(row <= col, factor[at, :], 0.0))
        fac_hi[at, :] = hi
        fac_lo[at, :] = lo
        return 0

    lax.fori_loop(0, C, split_factor, 0)
    alive = (grp < live[0]).astype(jnp.float32)

    def shift_copy(m):
        at = pl.ds(pl.multiple_of(m * H, H), H)
        return pltpu.make_async_remote_copy(
            solved.at[at], mine.at[at], shift_send.at[m], shift_recv.at[m],
            device_id=after, device_id_type=MESH,
        )

    def near_copy(side, m):
        at = pl.ds(pl.multiple_of(m * H, H), H)
        return pltpu.make_async_remote_copy(
            mine.at[at], gath.at[2 if side == 0 else 0, at],
            near_send.at[side, m], near_recv.at[side, m],
            device_id=up if side == 0 else down, device_id_type=MESH,
        )

    def fwd_copy(side, c):
        at = pl.ds(pl.multiple_of(c * R + side * H, H), H)
        return pltpu.make_async_remote_copy(
            gath.at[2 if side == 0 else 0, at], gath.at[1, at],
            fwd_send.at[side, c], fwd_recv.at[side, c],
            device_id=up if side == 0 else down, device_id_type=MESH,
        )

    def put_halves(slot, c, x):
        hi, lo = split(x)
        halves[slot, pl.ds(pl.multiple_of(c * 2 * R, 2 * R), R), :] = hi
        halves[slot, pl.ds(pl.multiple_of(c * 2 * R + R, R), R), :] = lo

    def solve_shift(c, _):
        at = pl.ds(pl.multiple_of(c * R, R), R)
        hi, lo = split(rows[at, :])
        both = jnp.concatenate([hi, lo], axis=0)
        for j in range(3):
            k = 256 * (j + 1)
            cols = pl.ds(256 * j, 256)
            x = jnp.dot(both[:, :k], fac_hi[pl.ds(0, k), cols], preferred_element_type=jnp.float32)
            y = jnp.dot(hi[:, :k], fac_lo[pl.ds(0, k), cols], preferred_element_type=jnp.float32)
            solved[at, cols] = alive * (x[:R] + (x[R:] + y))

        @pl.when(c < AHEAD)
        def _():
            shift_start(c)

        return 0

    def shift_start(c):
        shift_copy(2 * c).start()
        shift_copy(2 * c + 1).start()

    def near_start(c):
        @pl.when(c + AHEAD < C)
        def _():
            shift_start(c + AHEAD)

        shift_copy(2 * c).wait_recv()
        near_copy(0, 2 * c).start()
        shift_copy(2 * c + 1).wait_recv()
        near_copy(1, 2 * c + 1).start()
        near_copy(0, 2 * c + 1).start()
        near_copy(1, 2 * c).start()
        put_halves(0, c, mine[pl.ds(pl.multiple_of(c * R, R), R), :])

    def forward(c):
        near_copy(0, 2 * c).wait_recv()
        fwd_copy(0, c).start()
        near_copy(1, 2 * c + 1).wait_recv()
        fwd_copy(1, c).start()

    lax.fori_loop(0, C, solve_shift, 0)
    store_solved = pltpu.make_async_copy(solved, solved_out.at[0, 0], local_sem.at[0])
    store_solved.start()
    near_start(jnp.int32(0))
    pairs_copy.wait_recv()
    load_pairs = pltpu.make_async_copy(pairs_in, pairs, local_sem.at[2])
    load_pairs.start()
    load_pairs.wait()
    forward(0)
    near_start(jnp.int32(1))

    lefts = [lax.rem(pairs[0, p] - grp + 4, 4) for p in range(PAIRS)]
    rights = [lax.rem(pairs[1, p] - grp + 4, 4) for p in range(PAIRS)]
    dists = (1 + 2 * core, 3 - 2 * core, 0, 4, 2)
    weights = [
        [(pairs[2, p] == d).astype(jnp.float32) for p in range(PAIRS)] for d in dists
    ]

    def part_copy(n):
        return pltpu.make_async_remote_copy(
            out.at[n, pl.ds(0, 2)], part.at[n], part_send.at[n], part_recv.at[n],
            device_id=partner, device_id_type=MESH,
        )

    def low_copy(n):
        return pltpu.make_async_remote_copy(
            out.at[n, 2], xin.at[n, 0], low_send.at[n], low_recv.at[n],
            device_id=before, device_id_type=MESH,
        )

    def high_copy(n):
        return pltpu.make_async_remote_copy(
            out.at[n, 3], xin.at[n, 1], high_send.at[n], high_recv.at[n],
            device_id=after, device_id_type=MESH,
        )

    def combine_send(n):
        part_copy(n).wait_recv()
        out[n, 3 - core] = out[n, 3 - core] + part[n, 0]
        low_copy(n).start()
        high_copy(n).start()
        out[n, 4] = out[n, 4] + part[n, 1]

    def tile(c, k):
        n = c * c + k
        is_row = k <= c
        i = jnp.where(is_row, c, k - c - 1)
        j = jnp.where(is_row, k, c)
        at_i = pl.ds(pl.multiple_of(i * 2 * R, 2 * R), 2 * R)
        at_j = pl.ds(pl.multiple_of(j * 2 * R, 2 * R), 2 * R)
        for p in range(PAIRS):
            x = lax.dot_general(
                halves[lefts[p], at_i, :], halves[rights[p], at_j, :], NT,
                preferred_element_type=jnp.float32,
            )
            terms[p] = (x[:R, :R] + (x[R:, :R] + x[:R, R:])) + x[R:, R:]
        def mix(r, _):
            at = pl.ds(pl.multiple_of(r * 16, 16), 16)
            t = [terms[p, at, :] for p in range(PAIRS)]
            for slot in range(5):
                w = weights[slot]
                total = w[0] * t[0]
                for p in range(1, PAIRS):
                    total = total + w[p] * t[p]
                out[n, slot, at, :] = total
            return 0

        lax.fori_loop(0, R // 16, mix, 0, unroll=True)
        part_copy(n).start()

        @pl.when(k >= LAG)
        def _():
            combine_send(n - LAG)

    def finish(c):
        def one(k, _):
            n = c * c + k
            is_row = k <= c
            i = jnp.where(is_row, c, k - c - 1)
            j = jnp.where(is_row, k, c)
            at_i = pl.ds(pl.multiple_of(i * R, R), R)
            at_j = pl.ds(pl.multiple_of(j * R, R), R)
            low_copy(n).wait_recv()
            high_copy(n).wait_recv()
            upd[at_i, at_j] = base[at_i, at_j] - (out[n, 4] + (xin[n, 0] + xin[n, 1]))
            return 0

        lax.fori_loop(0, 2 * c + 1, one, 0)

    load_base.wait()

    def step(c, _):
        @pl.when(c >= 2)
        def _():
            finish(c - 2)

        at = pl.ds(pl.multiple_of(c * R, R), R)
        near_copy(0, 2 * c + 1).wait_recv()
        near_copy(1, 2 * c).wait_recv()
        put_halves(1, c, gath[0, at, :])
        put_halves(3, c, gath[2, at, :])
        fwd_copy(0, c).wait_recv()
        fwd_copy(1, c).wait_recv()
        put_halves(2, c, gath[1, at, :])

        def one_tile(k, _):
            tile(c, k)

            @pl.when(jnp.logical_and(k == jnp.minimum(MID, 2 * c), c + 1 < C))
            def _():
                forward(c + 1)

                @pl.when(c + 2 < C)
                def _():
                    near_start(c + 2)

            return 0

        lax.fori_loop(0, 2 * c + 1, one_tile, 0)

        def rest(k, _):
            combine_send(c * c + k)
            return 0

        lax.fori_loop(jnp.maximum(2 * c + 1 - LAG, 0), 2 * c + 1, rest, 0)
        return 0

    lax.fori_loop(0, C, step, 0)
    finish(C - 2)
    edge = B - R
    stores = [
        pltpu.make_async_copy(upd.at[pl.ds(r, h), pl.ds(c, w)], updated_out.at[0, 0, pl.ds(r, h), pl.ds(c, w)], sem)
        for r, h, c, w, sem in (
            (0, edge, 0, edge, local_sem.at[1]), (edge, R, 0, B, local_sem.at[2]), (0, edge, edge, R, local_sem.at[3])
        )
    ]
    stores[0].start()
    finish(C - 1)
    stores[1].start()
    stores[2].start()

    for group in range(4):
        @pl.when(grp < GROUPS[group][2])
        def _():
            for which, target in enumerate((up, down)):
                slab_copy(which, group, grp, target).wait_send()

        for side, slab in enumerate((below, above)):
            @pl.when(slab < GROUPS[group][2])
            def _():
                slab_fwd(side, group, slab).wait_send()

    pairs_copy.wait_send()

    def drain_piece(m, _):
        shift_copy(m).wait_send()
        for side in range(2):
            near_copy(side, m).wait_send()
        return 0

    def drain_chunk(c, _):
        for side in range(2):
            fwd_copy(side, c).wait_send()
        return 0

    def drain_tile(n, _):
        part_copy(n).wait_send()
        low_copy(n).wait_send()
        high_copy(n).wait_send()
        return 0

    lax.fori_loop(0, 2 * C, drain_piece, 0)
    lax.fori_loop(0, C, drain_chunk, 0)
    lax.fori_loop(0, TILES, drain_tile, 0)
    store_solved.wait()
    for store in stores:
        store.wait()


def shards(panel, diag_inverse, ancestor, live_blocks, pair_first, pair_second, pair_offset):
    f32, bf16 = jnp.float32, jnp.bfloat16
    dma = pltpu.SemaphoreType.DMA
    smem = pl.BlockSpec(memory_space=pltpu.SMEM)
    raw = pl.BlockSpec(memory_space=pl.ANY)
    block = jax.ShapeDtypeStruct((1, 1, B, B), f32)
    return pl.pallas_call(
        kernel,
        out_shape=(block, block),
        in_specs=[smem] * 4 + [raw] * 3,
        out_specs=(raw, raw),
        scratch_shapes=[
            pltpu.VMEM((B, B), f32),
            pltpu.VMEM((B, B), bf16),
            pltpu.VMEM((B, B), bf16),
            pltpu.VMEM((B, B), f32),
            pltpu.VMEM((B, B), f32),
            pltpu.VMEM((B, B), f32),
            pltpu.VMEM((3, B, B), f32),
            pltpu.VMEM((4, 2 * B, B), bf16),
            pltpu.VMEM((TILES, 5, R, R), f32),
            pltpu.VMEM((TILES, 2, R, R), f32),
            pltpu.VMEM((TILES, 2, R, R), f32),
            pltpu.VMEM((B, B), f32),
            pltpu.VMEM((B, B), f32),
            pltpu.VMEM((PAIRS, R, R), f32),
            pltpu.VMEM((8, 128), jnp.int32),
            pltpu.VMEM((8, 128), jnp.int32),
            pltpu.SMEM((8, 128), jnp.int32),
            dma((4,)),
            dma((2,)),
            dma((4, 4)),
            dma((4, 4)),
            dma((2 * C,)),
            dma((2 * C,)),
            dma((2, 2 * C)),
            dma((2, 2 * C)),
            dma((2, C)),
            dma((2, C)),
            dma((TILES,)),
            dma((TILES,)),
            dma((TILES,)),
            dma((TILES,)),
            dma((TILES,)),
            dma((TILES,)),
        ],
        compiler_params=pltpu.CompilerParams(
            collective_id=0, has_side_effects=True, vmem_limit_bytes=60 * 2**20
        ),
    )(live_blocks, pair_first, pair_second, pair_offset, panel, diag_inverse, ancestor)


def solution(mesh):
    placed = (
        P("own", "grp", None, None),
        P("own", "grp", None),
        P("own", "grp", None, None),
        P("own"),
        P("own", "grp", None),
        P("own", "grp", None),
        P("own", "grp", None),
    )
    return jax.shard_map(
        shards,
        mesh=mesh,
        in_specs=placed,
        out_specs=(P("own", "grp", None, None), P("own", "grp", None, None)),
        check_vma=False,
    )
```

```python
import jax
import jax.numpy as jnp
from jax import lax
from jax.experimental import pallas as pl
from jax.experimental.pallas import tpu as pltpu
from jax.sharding import PartitionSpec as P

MESH = pl.DeviceIdType.MESH
B = 768
PAIRS = 7
R = 128
C = B // R
H = R // 2
Q = R // 4
TILES = C * C
MID = 4
AHEAD = 2
LAG = 2
SLAB = B // 4
GROUPS = ((0, 128, 1), (128, 256, 2), (384, 128, 3), (512, 256, 4))
NT = (((1,), (1,)), ((), ()))


def split(x):
    hi = x.astype(jnp.bfloat16)
    lo = (x - hi.astype(jnp.float32)).astype(jnp.bfloat16)
    return hi, lo


def kernel(
    live, first, second, offset, panel, diag, anc,
    solved_out, updated_out,
    factor, fac_hi, fac_lo, rows, solved, mine, gath, halves, out, part, xin, base, upd, terms,
    packed, pairs_in, pairs, local_sem, pairs_sem, fac_send, fac_recv, shift_send, shift_recv,
    near_send, near_recv, fwd_send, fwd_recv, part_send, part_recv, low_send, low_recv, high_send, high_recv,
):
    own = lax.axis_index("own")
    grp = lax.axis_index("grp")
    core = lax.rem(own, 2)

    def dev(by_own, by_grp):
        return (lax.rem(own + by_own + 64, 64), lax.rem(grp + by_grp + 4, 4))

    partner = (own + 1 - 2 * core, grp)
    up, down = dev(0, 1), dev(0, -1)

    load_rows = pltpu.make_async_copy(panel.at[0, 0], rows, local_sem.at[0])
    load_base = pltpu.make_async_copy(anc.at[0, 0], base, local_sem.at[1])
    load_rows.start()
    load_base.start()
    barrier = pltpu.get_barrier_semaphore()
    after, before = dev(2, 0), dev(-2, 0)
    peers = (up, down, partner, after, before)
    for peer in peers:
        pl.semaphore_signal(barrier, 1, device_id=peer, device_id_type=MESH)
    pl.semaphore_wait(barrier, len(peers))

    def slab_fwd(side, group, slab):
        start, width, _ = GROUPS[group]
        at = pl.multiple_of(slab * SLAB + side * (SLAB // 2), SLAB // 2)
        place = factor.at[pl.ds(at, SLAB // 2), pl.ds(start, width)]
        return pltpu.make_async_remote_copy(
            place, place, fac_send.at[2 + side, group], fac_recv.at[2 + side, group],
            device_id=up if side == 0 else down, device_id_type=MESH,
        )

    def slab_copy(which, group, source_slab, target):
        start, width, _ = GROUPS[group]
        place = factor.at[pl.ds(pl.multiple_of(source_slab * SLAB, SLAB), SLAB), pl.ds(start, width)]
        return pltpu.make_async_remote_copy(
            diag.at[0, :, pl.ds(start, width)], place,
            fac_send.at[which, group], fac_recv.at[which, group],
            device_id=target, device_id_type=MESH,
        )

    for group in (3, 1, 2, 0):
        @pl.when(grp < GROUPS[group][2])
        def _():
            for which, target in enumerate((up, down)):
                slab_copy(which, group, grp, target).start()

    spot = lax.broadcasted_iota(jnp.int32, (8, 128), 1) + 128 * lax.broadcasted_iota(jnp.int32, (8, 128), 0)
    values = jnp.zeros((8, 128), jnp.int32)
    for row, source in enumerate((first, second, offset)):
        for p in range(PAIRS):
            values = jnp.where(spot == 128 * row + p, source[0, 0, p], values)
    packed[...] = values
    pairs_copy = pltpu.make_async_remote_copy(
        packed, pairs_in, pairs_sem.at[0], pairs_sem.at[1], device_id=after, device_id_type=MESH
    )
    pairs_copy.start()

    load_slab = pltpu.make_async_copy(
        diag.at[0], factor.at[pl.ds(pl.multiple_of(grp * SLAB, SLAB), SLAB)], local_sem.at[2]
    )
    load_slab.start()
    below, above, opposite = (lax.rem(grp + by, 4) for by in (3, 1, 2))
    for group in (3, 1, 2, 0):
        for side, slab in enumerate((below, above)):
            @pl.when(slab < GROUPS[group][2])
            def _():
                slab_copy(side, group, slab, up).wait_recv()
                slab_fwd(side, group, slab).start()

    load_slab.wait()
    for group in (3, 1, 2, 0):
        @pl.when(opposite < GROUPS[group][2])
        def _():
            for side in range(2):
                slab_fwd(side, group, opposite).wait_recv()
    load_rows.wait()

    def split_factor(c, _):
        at = pl.ds(pl.multiple_of(c * R, R), R)
        row = lax.broadcasted_iota(jnp.int32, (R, B), 0) + c * R
        col = lax.broadcasted_iota(jnp.int32, (R, B), 1)
        hi, lo = split(jnp.where(row <= col, factor[at, :], 0.0))
        fac_hi[at, :] = hi
        fac_lo[at, :] = lo
        return 0

    lax.fori_loop(0, C, split_factor, 0)
    alive = (grp < live[0]).astype(jnp.float32)

    def shift_copy(m):
        at = pl.ds(pl.multiple_of(m * Q, Q), Q)
        return pltpu.make_async_remote_copy(
            solved.at[at], mine.at[at], shift_send.at[m], shift_recv.at[m],
            device_id=after, device_id_type=MESH,
        )

    def near_copy(side, m):
        at = pl.ds(pl.multiple_of(m * Q, Q), Q)
        return pltpu.make_async_remote_copy(
            mine.at[at], gath.at[2 if side == 0 else 0, at],
            near_send.at[side, m], near_recv.at[side, m],
            device_id=up if side == 0 else down, device_id_type=MESH,
        )

    def fwd_copy(side, c):
        at = pl.ds(pl.multiple_of(c * R + side * H, H), H)
        return pltpu.make_async_remote_copy(
            gath.at[2 if side == 0 else 0, at], gath.at[1, at],
            fwd_send.at[side, c], fwd_recv.at[side, c],
            device_id=up if side == 0 else down, device_id_type=MESH,
        )

    def put_halves(slot, c, x):
        hi, lo = split(x)
        halves[slot, pl.ds(pl.multiple_of(c * 2 * R, 2 * R), R), :] = hi
        halves[slot, pl.ds(pl.multiple_of(c * 2 * R + R, R), R), :] = lo

    def solve_shift(c, _):
        at = pl.ds(pl.multiple_of(c * R, R), R)
        hi, lo = split(rows[at, :])
        both = jnp.concatenate([hi, lo], axis=0)
        for j in range(3):
            k = 256 * (j + 1)
            cols = pl.ds(256 * j, 256)
            x = jnp.dot(both[:, :k], fac_hi[pl.ds(0, k), cols], preferred_element_type=jnp.float32)
            y = jnp.dot(hi[:, :k], fac_lo[pl.ds(0, k), cols], preferred_element_type=jnp.float32)
            solved[at, cols] = alive * (x[:R] + (x[R:] + y))

        @pl.when(c < AHEAD)
        def _():
            shift_start(c)

        return 0

    def shift_start(c):
        for q in (0, 2, 1, 3):
            shift_copy(4 * c + q).start()

    def near_start(c):
        @pl.when(c + AHEAD < C)
        def _():
            shift_start(c + AHEAD)

        for side, q in ((0, 0), (1, 2), (0, 1), (1, 3)):
            shift_copy(4 * c + q).wait_recv()
            near_copy(side, 4 * c + q).start()
        for side, q in ((0, 2), (1, 0), (0, 3), (1, 1)):
            near_copy(side, 4 * c + q).start()
        put_halves(0, c, mine[pl.ds(pl.multiple_of(c * R, R), R), :])

    def forward(c):
        for side in range(2):
            for q in range(2):
                near_copy(side, 4 * c + 2 * side + q).wait_recv()
            fwd_copy(side, c).start()

    lax.fori_loop(0, C, solve_shift, 0)
    store_solved = pltpu.make_async_copy(solved, solved_out.at[0, 0], local_sem.at[0])
    store_solved.start()
    near_start(jnp.int32(0))
    pairs_copy.wait_recv()
    load_pairs = pltpu.make_async_copy(pairs_in, pairs, local_sem.at[2])
    load_pairs.start()
    load_pairs.wait()
    forward(0)
    near_start(jnp.int32(1))

    lefts = [lax.rem(pairs[0, p] - grp + 4, 4) for p in range(PAIRS)]
    rights = [lax.rem(pairs[1, p] - grp + 4, 4) for p in range(PAIRS)]
    dists = (1 + 2 * core, 3 - 2 * core, 0, 4, 2)
    weights = [
        [(pairs[2, p] == d).astype(jnp.float32) for p in range(PAIRS)] for d in dists
    ]

    def part_copy(n):
        return pltpu.make_async_remote_copy(
            out.at[n, pl.ds(0, 2)], part.at[n], part_send.at[n], part_recv.at[n],
            device_id=partner, device_id_type=MESH,
        )

    def low_copy(n):
        return pltpu.make_async_remote_copy(
            out.at[n, 2], xin.at[n, 0], low_send.at[n], low_recv.at[n],
            device_id=before, device_id_type=MESH,
        )

    def high_copy(n):
        return pltpu.make_async_remote_copy(
            out.at[n, 3], xin.at[n, 1], high_send.at[n], high_recv.at[n],
            device_id=after, device_id_type=MESH,
        )

    def combine_send(n):
        part_copy(n).wait_recv()
        out[n, 3 - core] = out[n, 3 - core] + part[n, 0]
        low_copy(n).start()
        high_copy(n).start()
        out[n, 4] = out[n, 4] + part[n, 1]

    def tile(c, k):
        n = c * c + k
        is_row = k <= c
        i = jnp.where(is_row, c, k - c - 1)
        j = jnp.where(is_row, k, c)
        at_i = pl.ds(pl.multiple_of(i * 2 * R, 2 * R), 2 * R)
        at_j = pl.ds(pl.multiple_of(j * 2 * R, 2 * R), 2 * R)
        for p in range(PAIRS):
            x = lax.dot_general(
                halves[lefts[p], at_i, :], halves[rights[p], at_j, :], NT,
                preferred_element_type=jnp.float32,
            )
            terms[p] = (x[:R, :R] + (x[R:, :R] + x[:R, R:])) + x[R:, R:]
        def mix(r, _):
            at = pl.ds(pl.multiple_of(r * 16, 16), 16)
            t = [terms[p, at, :] for p in range(PAIRS)]
            for slot in range(5):
                w = weights[slot]
                total = w[0] * t[0]
                for p in range(1, PAIRS):
                    total = total + w[p] * t[p]
                out[n, slot, at, :] = total
            return 0

        lax.fori_loop(0, R // 16, mix, 0, unroll=True)
        part_copy(n).start()

        @pl.when(k >= LAG)
        def _():
            combine_send(n - LAG)

    def finish(c):
        def one(k, _):
            n = c * c + k
            is_row = k <= c
            i = jnp.where(is_row, c, k - c - 1)
            j = jnp.where(is_row, k, c)
            at_i = pl.ds(pl.multiple_of(i * R, R), R)
            at_j = pl.ds(pl.multiple_of(j * R, R), R)
            low_copy(n).wait_recv()
            high_copy(n).wait_recv()
            upd[at_i, at_j] = base[at_i, at_j] - (out[n, 4] + (xin[n, 0] + xin[n, 1]))
            return 0

        lax.fori_loop(0, 2 * c + 1, one, 0)

    load_base.wait()

    def step(c, _):
        @pl.when(c >= 2)
        def _():
            finish(c - 2)

        at = pl.ds(pl.multiple_of(c * R, R), R)
        for side in range(2):
            for q in range(2):
                near_copy(side, 4 * c + 2 * (1 - side) + q).wait_recv()
        put_halves(1, c, gath[0, at, :])
        put_halves(3, c, gath[2, at, :])
        fwd_copy(0, c).wait_recv()
        fwd_copy(1, c).wait_recv()
        put_halves(2, c, gath[1, at, :])

        def one_tile(k, _):
            tile(c, k)

            @pl.when(jnp.logical_and(k == jnp.minimum(MID, 2 * c), c + 1 < C))
            def _():
                forward(c + 1)

                @pl.when(c + 2 < C)
                def _():
                    near_start(c + 2)

            return 0

        lax.fori_loop(0, 2 * c + 1, one_tile, 0)

        def rest(k, _):
            combine_send(c * c + k)
            return 0

        lax.fori_loop(jnp.maximum(2 * c + 1 - LAG, 0), 2 * c + 1, rest, 0)
        return 0

    lax.fori_loop(0, C, step, 0)
    finish(C - 2)
    edge = B - R
    stores = [
        pltpu.make_async_copy(upd.at[pl.ds(r, h), pl.ds(c, w)], updated_out.at[0, 0, pl.ds(r, h), pl.ds(c, w)], sem)
        for r, h, c, w, sem in (
            (0, edge, 0, edge, local_sem.at[1]), (edge, R, 0, B, local_sem.at[2]), (0, edge, edge, R, local_sem.at[3])
        )
    ]
    stores[0].start()
    for group in range(4):
        @pl.when(grp < GROUPS[group][2])
        def _():
            for which, target in enumerate((up, down)):
                slab_copy(which, group, grp, target).wait_send()

        for side, slab in enumerate((below, above)):
            @pl.when(slab < GROUPS[group][2])
            def _():
                slab_fwd(side, group, slab).wait_send()

    pairs_copy.wait_send()

    def drain_piece(m, _):
        shift_copy(m).wait_send()
        for side in range(2):
            near_copy(side, m).wait_send()
        return 0

    def drain_chunk(c, _):
        for side in range(2):
            fwd_copy(side, c).wait_send()
        return 0

    def drain_part(n, _):
        part_copy(n).wait_send()
        return 0

    def drain_tile(n, _):
        low_copy(n).wait_send()
        high_copy(n).wait_send()
        return 0

    lax.fori_loop(0, 4 * C, drain_piece, 0)
    lax.fori_loop(0, C, drain_chunk, 0)
    lax.fori_loop(0, TILES, drain_part, 0)
    lax.fori_loop(0, (C - 1) * (C - 1), drain_tile, 0)
    store_solved.wait()
    finish(C - 1)
    stores[1].start()
    stores[2].start()
    lax.fori_loop((C - 1) * (C - 1), TILES, drain_tile, 0)
    for store in stores:
        store.wait()


def shards(panel, diag_inverse, ancestor, live_blocks, pair_first, pair_second, pair_offset):
    f32, bf16 = jnp.float32, jnp.bfloat16
    dma = pltpu.SemaphoreType.DMA
    smem = pl.BlockSpec(memory_space=pltpu.SMEM)
    raw = pl.BlockSpec(memory_space=pl.ANY)
    block = jax.ShapeDtypeStruct((1, 1, B, B), f32)
    return pl.pallas_call(
        kernel,
        out_shape=(block, block),
        in_specs=[smem] * 4 + [raw] * 3,
        out_specs=(raw, raw),
        scratch_shapes=[
            pltpu.VMEM((B, B), f32),
            pltpu.VMEM((B, B), bf16),
            pltpu.VMEM((B, B), bf16),
            pltpu.VMEM((B, B), f32),
            pltpu.VMEM((B, B), f32),
            pltpu.VMEM((B, B), f32),
            pltpu.VMEM((3, B, B), f32),
            pltpu.VMEM((4, 2 * B, B), bf16),
            pltpu.VMEM((TILES, 5, R, R), f32),
            pltpu.VMEM((TILES, 2, R, R), f32),
            pltpu.VMEM((TILES, 2, R, R), f32),
            pltpu.VMEM((B, B), f32),
            pltpu.VMEM((B, B), f32),
            pltpu.VMEM((PAIRS, R, R), f32),
            pltpu.VMEM((8, 128), jnp.int32),
            pltpu.VMEM((8, 128), jnp.int32),
            pltpu.SMEM((8, 128), jnp.int32),
            dma((4,)),
            dma((2,)),
            dma((4, 4)),
            dma((4, 4)),
            dma((4 * C,)),
            dma((4 * C,)),
            dma((2, 4 * C)),
            dma((2, 4 * C)),
            dma((2, C)),
            dma((2, C)),
            dma((TILES,)),
            dma((TILES,)),
            dma((TILES,)),
            dma((TILES,)),
            dma((TILES,)),
            dma((TILES,)),
        ],
        compiler_params=pltpu.CompilerParams(
            collective_id=0, has_side_effects=True, vmem_limit_bytes=60 * 2**20
        ),
    )(live_blocks, pair_first, pair_second, pair_offset, panel, diag_inverse, ancestor)


def solution(mesh):
    placed = (
        P("own", "grp", None, None),
        P("own", "grp", None),
        P("own", "grp", None, None),
        P("own"),
        P("own", "grp", None),
        P("own", "grp", None),
        P("own", "grp", None),
    )
    return jax.shard_map(
        shards,
        mesh=mesh,
        in_specs=placed,
        out_specs=(P("own", "grp", None, None), P("own", "grp", None, None)),
        check_vma=False,
    )
```

```python
import jax
import jax.numpy as jnp
from jax import lax
from jax.experimental import pallas as pl
from jax.experimental.pallas import tpu as pltpu
from jax.sharding import PartitionSpec as P

MESH = pl.DeviceIdType.MESH
B = 768
PAIRS = 7
R = 128
C = B // R
H = R // 2
Q = R // 4
TILES = C * C
MID = 4
AHEAD = 2
LAG = 2
SLAB = B // 4
GROUPS = ((0, 128, 1), (128, 256, 2), (384, 128, 3), (512, 256, 4))
NT = (((1,), (1,)), ((), ()))


def split(x):
    hi = x.astype(jnp.bfloat16)
    lo = (x - hi.astype(jnp.float32)).astype(jnp.bfloat16)
    return hi, lo


def kernel(
    live, first, second, offset, panel, diag, anc,
    solved_out, updated_out,
    factor, fac_hi, fac_lo, rows, solved, mine, gath, halves, out, part, xin, base, upd, terms,
    packed, pairs_in, pairs, local_sem, pairs_sem, fac_send, fac_recv, shift_send, shift_recv,
    near_send, near_recv, fwd_send, fwd_recv, part_send, part_recv, low_send, low_recv, high_send, high_recv,
):
    own = lax.axis_index("own")
    grp = lax.axis_index("grp")
    core = lax.rem(own, 2)

    def dev(by_own, by_grp):
        return (lax.rem(own + by_own + 64, 64), lax.rem(grp + by_grp + 4, 4))

    partner = (own + 1 - 2 * core, grp)
    up, down = dev(0, 1), dev(0, -1)

    load_rows = pltpu.make_async_copy(panel.at[0, 0], rows, local_sem.at[0])
    load_base = pltpu.make_async_copy(anc.at[0, 0], base, local_sem.at[1])
    load_rows.start()
    load_base.start()
    barrier = pltpu.get_barrier_semaphore()
    after, before = dev(2, 0), dev(-2, 0)
    peers = (up, down, partner, after, before)
    for peer in peers:
        pl.semaphore_signal(barrier, 1, device_id=peer, device_id_type=MESH)
    pl.semaphore_wait(barrier, len(peers))

    def slab_fwd(side, group, slab):
        start, width, _ = GROUPS[group]
        at = pl.multiple_of(slab * SLAB + side * (SLAB // 2), SLAB // 2)
        place = factor.at[pl.ds(at, SLAB // 2), pl.ds(start, width)]
        return pltpu.make_async_remote_copy(
            place, place, fac_send.at[2 + side, group], fac_recv.at[2 + side, group],
            device_id=up if side == 0 else down, device_id_type=MESH,
        )

    def slab_copy(which, group, source_slab, target):
        start, width, _ = GROUPS[group]
        place = factor.at[pl.ds(pl.multiple_of(source_slab * SLAB, SLAB), SLAB), pl.ds(start, width)]
        return pltpu.make_async_remote_copy(
            diag.at[0, :, pl.ds(start, width)], place,
            fac_send.at[which, group], fac_recv.at[which, group],
            device_id=target, device_id_type=MESH,
        )

    for group in (3, 1, 2, 0):
        @pl.when(grp < GROUPS[group][2])
        def _():
            for which, target in enumerate((up, down)):
                slab_copy(which, group, grp, target).start()

    spot = lax.broadcasted_iota(jnp.int32, (8, 128), 1) + 128 * lax.broadcasted_iota(jnp.int32, (8, 128), 0)
    values = jnp.zeros((8, 128), jnp.int32)
    for row, source in enumerate((first, second, offset)):
        for p in range(PAIRS):
            values = jnp.where(spot == 128 * row + p, source[0, 0, p], values)
    packed[...] = values
    pairs_copy = pltpu.make_async_remote_copy(
        packed, pairs_in, pairs_sem.at[0], pairs_sem.at[1], device_id=after, device_id_type=MESH
    )
    pairs_copy.start()

    load_slab = pltpu.make_async_copy(
        diag.at[0], factor.at[pl.ds(pl.multiple_of(grp * SLAB, SLAB), SLAB)], local_sem.at[2]
    )
    load_slab.start()
    below, above, opposite = (lax.rem(grp + by, 4) for by in (3, 1, 2))
    for group in (3, 1, 2, 0):
        for side, slab in enumerate((below, above)):
            @pl.when(slab < GROUPS[group][2])
            def _():
                slab_copy(side, group, slab, up).wait_recv()
                slab_fwd(side, group, slab).start()

    load_slab.wait()
    for group in (3, 1, 2, 0):
        @pl.when(opposite < GROUPS[group][2])
        def _():
            for side in range(2):
                slab_fwd(side, group, opposite).wait_recv()
    load_rows.wait()

    def split_factor(c, _):
        at = pl.ds(pl.multiple_of(c * R, R), R)
        row = lax.broadcasted_iota(jnp.int32, (R, B), 0) + c * R
        col = lax.broadcasted_iota(jnp.int32, (R, B), 1)
        hi, lo = split(jnp.where(row <= col, factor[at, :], 0.0))
        fac_hi[at, :] = hi
        fac_lo[at, :] = lo
        return 0

    lax.fori_loop(0, C, split_factor, 0)
    alive = (grp < live[0]).astype(jnp.float32)

    def shift_copy(m):
        at = pl.ds(pl.multiple_of(m * Q, Q), Q)
        return pltpu.make_async_remote_copy(
            solved.at[at], mine.at[at], shift_send.at[m], shift_recv.at[m],
            device_id=after, device_id_type=MESH,
        )

    def near_copy(side, m):
        at = pl.ds(pl.multiple_of(m * Q, Q), Q)
        return pltpu.make_async_remote_copy(
            mine.at[at], gath.at[2 if side == 0 else 0, at],
            near_send.at[side, m], near_recv.at[side, m],
            device_id=up if side == 0 else down, device_id_type=MESH,
        )

    def fwd_copy(side, c):
        at = pl.ds(pl.multiple_of(c * R + side * H, H), H)
        return pltpu.make_async_remote_copy(
            gath.at[2 if side == 0 else 0, at], gath.at[1, at],
            fwd_send.at[side, c], fwd_recv.at[side, c],
            device_id=up if side == 0 else down, device_id_type=MESH,
        )

    def put_halves(slot, c, x):
        hi, lo = split(x)
        halves[slot, pl.ds(pl.multiple_of(c * 2 * R, 2 * R), R), :] = hi
        halves[slot, pl.ds(pl.multiple_of(c * 2 * R + R, R), R), :] = lo

    def solve_shift(c, _):
        at = pl.ds(pl.multiple_of(c * R, R), R)
        hi, lo = split(rows[at, :])
        both = jnp.concatenate([hi, lo], axis=0)
        for j in range(3):
            k = 256 * (j + 1)
            cols = pl.ds(256 * j, 256)
            x = jnp.dot(both[:, :k], fac_hi[pl.ds(0, k), cols], preferred_element_type=jnp.float32)
            y = jnp.dot(hi[:, :k], fac_lo[pl.ds(0, k), cols], preferred_element_type=jnp.float32)
            solved[at, cols] = alive * (x[:R] + (x[R:] + y))

        @pl.when(c < AHEAD)
        def _():
            shift_start(c)

        return 0

    def shift_start(c):
        for q in (0, 2, 1, 3):
            shift_copy(4 * c + q).start()

    def near_start(c):
        @pl.when(c + AHEAD < C)
        def _():
            shift_start(c + AHEAD)

        for side, q in ((0, 0), (1, 2), (0, 1), (1, 3)):
            shift_copy(4 * c + q).wait_recv()
            near_copy(side, 4 * c + q).start()
        for side, q in ((0, 2), (1, 0), (0, 3), (1, 1)):
            near_copy(side, 4 * c + q).start()
        put_halves(0, c, mine[pl.ds(pl.multiple_of(c * R, R), R), :])

    def forward(c):
        for side in range(2):
            for q in range(2):
                near_copy(side, 4 * c + 2 * side + q).wait_recv()
            fwd_copy(side, c).start()

    lax.fori_loop(0, C, solve_shift, 0)
    store_solved = pltpu.make_async_copy(solved, solved_out.at[0, 0], local_sem.at[0])
    store_solved.start()
    near_start(jnp.int32(0))
    pairs_copy.wait_recv()
    load_pairs = pltpu.make_async_copy(pairs_in, pairs, local_sem.at[2])
    load_pairs.start()
    load_pairs.wait()
    forward(0)
    near_start(jnp.int32(1))

    lefts = [lax.rem(pairs[0, p] - grp + 4, 4) for p in range(PAIRS)]
    rights = [lax.rem(pairs[1, p] - grp + 4, 4) for p in range(PAIRS)]
    dists = (1 + 2 * core, 3 - 2 * core, 0, 4, 2)
    weights = [
        [(pairs[2, p] == d).astype(jnp.float32) for p in range(PAIRS)] for d in dists
    ]

    def part_copy(n):
        return pltpu.make_async_remote_copy(
            out.at[n, pl.ds(0, 2)], part.at[n], part_send.at[n], part_recv.at[n],
            device_id=partner, device_id_type=MESH,
        )

    def low_copy(n):
        return pltpu.make_async_remote_copy(
            out.at[n, 2], xin.at[n, 0], low_send.at[n], low_recv.at[n],
            device_id=before, device_id_type=MESH,
        )

    def high_copy(n):
        return pltpu.make_async_remote_copy(
            out.at[n, 3], xin.at[n, 1], high_send.at[n], high_recv.at[n],
            device_id=after, device_id_type=MESH,
        )

    def combine_send(n):
        part_copy(n).wait_recv()
        out[n, 3 - core] = out[n, 3 - core] + part[n, 0]
        low_copy(n).start()
        high_copy(n).start()
        out[n, 4] = out[n, 4] + part[n, 1]

    def tile(c, k):
        n = c * c + k
        is_row = k <= c
        i = jnp.where(is_row, c, k - c - 1)
        j = jnp.where(is_row, k, c)
        at_i = pl.ds(pl.multiple_of(i * 2 * R, 2 * R), 2 * R)
        at_j = pl.ds(pl.multiple_of(j * 2 * R, 2 * R), 2 * R)
        for p in range(PAIRS):
            x = lax.dot_general(
                halves[lefts[p], at_i, :], halves[rights[p], at_j, :], NT,
                preferred_element_type=jnp.float32,
            )
            terms[p] = (x[:R, :R] + (x[R:, :R] + x[:R, R:])) + x[R:, R:]
            if p == 2:
                @pl.when(k >= LAG)
                def _():
                    combine_send(n - LAG)

        def mix(r, _):
            at = pl.ds(pl.multiple_of(r * 16, 16), 16)
            t = [terms[p, at, :] for p in range(PAIRS)]
            for slot in range(5):
                w = weights[slot]
                total = w[0] * t[0]
                for p in range(1, PAIRS):
                    total = total + w[p] * t[p]
                out[n, slot, at, :] = total
            return 0

        lax.fori_loop(0, R // 16, mix, 0, unroll=True)
        part_copy(n).start()


    def finish(c):
        def one(k, _):
            n = c * c + k
            is_row = k <= c
            i = jnp.where(is_row, c, k - c - 1)
            j = jnp.where(is_row, k, c)
            at_i = pl.ds(pl.multiple_of(i * R, R), R)
            at_j = pl.ds(pl.multiple_of(j * R, R), R)
            low_copy(n).wait_recv()
            high_copy(n).wait_recv()
            upd[at_i, at_j] = base[at_i, at_j] - (out[n, 4] + (xin[n, 0] + xin[n, 1]))
            return 0

        lax.fori_loop(0, 2 * c + 1, one, 0)

    load_base.wait()

    def step(c, _):
        @pl.when(c >= 2)
        def _():
            finish(c - 2)

        at = pl.ds(pl.multiple_of(c * R, R), R)
        for side in range(2):
            for q in range(2):
                near_copy(side, 4 * c + 2 * (1 - side) + q).wait_recv()
        put_halves(1, c, gath[0, at, :])
        put_halves(3, c, gath[2, at, :])
        fwd_copy(0, c).wait_recv()
        fwd_copy(1, c).wait_recv()
        put_halves(2, c, gath[1, at, :])

        def one_tile(k, _):
            tile(c, k)

            @pl.when(jnp.logical_and(k == jnp.minimum(MID, 2 * c), c + 1 < C))
            def _():
                forward(c + 1)

                @pl.when(c + 2 < C)
                def _():
                    near_start(c + 2)

            return 0

        lax.fori_loop(0, 2 * c + 1, one_tile, 0)

        def rest(k, _):
            combine_send(c * c + k)
            return 0

        lax.fori_loop(jnp.maximum(2 * c + 1 - LAG, 0), 2 * c + 1, rest, 0)
        return 0

    lax.fori_loop(0, C, step, 0)
    finish(C - 2)
    edge = B - R
    stores = [
        pltpu.make_async_copy(upd.at[pl.ds(r, h), pl.ds(c, w)], updated_out.at[0, 0, pl.ds(r, h), pl.ds(c, w)], sem)
        for r, h, c, w, sem in (
            (0, edge, 0, edge, local_sem.at[1]), (edge, R, 0, B, local_sem.at[2]), (0, edge, edge, R, local_sem.at[3])
        )
    ]
    stores[0].start()
    for group in range(4):
        @pl.when(grp < GROUPS[group][2])
        def _():
            for which, target in enumerate((up, down)):
                slab_copy(which, group, grp, target).wait_send()

        for side, slab in enumerate((below, above)):
            @pl.when(slab < GROUPS[group][2])
            def _():
                slab_fwd(side, group, slab).wait_send()

    pairs_copy.wait_send()

    def drain_piece(m, _):
        shift_copy(m).wait_send()
        for side in range(2):
            near_copy(side, m).wait_send()
        return 0

    def drain_chunk(c, _):
        for side in range(2):
            fwd_copy(side, c).wait_send()
        return 0

    def drain_part(n, _):
        part_copy(n).wait_send()
        return 0

    def drain_tile(n, _):
        low_copy(n).wait_send()
        high_copy(n).wait_send()
        return 0

    lax.fori_loop(0, 4 * C, drain_piece, 0)
    lax.fori_loop(0, C, drain_chunk, 0)
    lax.fori_loop(0, TILES, drain_part, 0)
    lax.fori_loop(0, (C - 1) * (C - 1), drain_tile, 0)
    store_solved.wait()
    finish(C - 1)
    stores[1].start()
    stores[2].start()
    lax.fori_loop((C - 1) * (C - 1), TILES, drain_tile, 0)
    for store in stores:
        store.wait()


def shards(panel, diag_inverse, ancestor, live_blocks, pair_first, pair_second, pair_offset):
    f32, bf16 = jnp.float32, jnp.bfloat16
    dma = pltpu.SemaphoreType.DMA
    smem = pl.BlockSpec(memory_space=pltpu.SMEM)
    raw = pl.BlockSpec(memory_space=pl.ANY)
    block = jax.ShapeDtypeStruct((1, 1, B, B), f32)
    return pl.pallas_call(
        kernel,
        out_shape=(block, block),
        in_specs=[smem] * 4 + [raw] * 3,
        out_specs=(raw, raw),
        scratch_shapes=[
            pltpu.VMEM((B, B), f32),
            pltpu.VMEM((B, B), bf16),
            pltpu.VMEM((B, B), bf16),
            pltpu.VMEM((B, B), f32),
            pltpu.VMEM((B, B), f32),
            pltpu.VMEM((B, B), f32),
            pltpu.VMEM((3, B, B), f32),
            pltpu.VMEM((4, 2 * B, B), bf16),
            pltpu.VMEM((TILES, 5, R, R), f32),
            pltpu.VMEM((TILES, 2, R, R), f32),
            pltpu.VMEM((TILES, 2, R, R), f32),
            pltpu.VMEM((B, B), f32),
            pltpu.VMEM((B, B), f32),
            pltpu.VMEM((PAIRS, R, R), f32),
            pltpu.VMEM((8, 128), jnp.int32),
            pltpu.VMEM((8, 128), jnp.int32),
            pltpu.SMEM((8, 128), jnp.int32),
            dma((4,)),
            dma((2,)),
            dma((4, 4)),
            dma((4, 4)),
            dma((4 * C,)),
            dma((4 * C,)),
            dma((2, 4 * C)),
            dma((2, 4 * C)),
            dma((2, C)),
            dma((2, C)),
            dma((TILES,)),
            dma((TILES,)),
            dma((TILES,)),
            dma((TILES,)),
            dma((TILES,)),
            dma((TILES,)),
        ],
        compiler_params=pltpu.CompilerParams(
            collective_id=0, has_side_effects=True, vmem_limit_bytes=60 * 2**20
        ),
    )(live_blocks, pair_first, pair_second, pair_offset, panel, diag_inverse, ancestor)


def solution(mesh):
    placed = (
        P("own", "grp", None, None),
        P("own", "grp", None),
        P("own", "grp", None, None),
        P("own"),
        P("own", "grp", None),
        P("own", "grp", None),
        P("own", "grp", None),
    )
    return jax.shard_map(
        shards,
        mesh=mesh,
        in_specs=placed,
        out_specs=(P("own", "grp", None, None), P("own", "grp", None, None)),
        check_vma=False,
    )
```
